32 devices in a mesh: client: 4 (over x, core), blk: 8 (over z, y).
Axes of the slice: x: 2, y: 2, z: 4, core: 2. Of those that a mesh axis runs over, the one named last changes fastest.
Arguments:
- activations: bfloat16 [8, 2, 8, 8, 1280], P('client', None, 'blk'), may hold values from -6 to 6
- sample_count: int32 [8], replicated, may hold values from 1 to 2, as said below
- client_weights: bfloat16 [8, 11520, 1280], P('client', 'blk'), may hold values from -6 to 6
Outputs:
- merged_gram: float32 [11520, 11520], P(('blk', 'client'))
- merged_rhs: float32 [11520, 1280], P(('blk', 'client'))
The draws below stay inside these ranges and needn't reach their ends.
Inputs may be any that keep to these rules, and one draw needn't show every extreme that they name: `sample_count`: some client has all 2 slots live in every draw.
All inputs are finite; a program needn't handle non-finite values.
Results may differ from the reference program's by a relative error of at most 0.0029.
Values may be sent and summed in bfloat16 or wider, within the bound.
A program may use at most 192 MiB of HBM per device.

```python
import jax
import jax.numpy as jnp
from jax import lax

CH = 1280
COUT = 1280
IMG_W = 8
SLOTS = 2
CLIENTS = 8
HH = 8
KK = 11520


def draw_sample_count(key, part):
    first_key, second_key = jax.random.split(jax.random.fold_in(key, 17))
    counts_drawn = jax.random.randint(first_key, (CLIENTS,), 1, SLOTS + 1)
    filled_client = jax.random.randint(second_key, (), 0, CLIENTS)
    positions = jnp.arange(CLIENTS)
    return jnp.where(positions == filled_client, SLOTS, counts_drawn).astype(jnp.int32)


def block_levels(own_key, extent, cuts, low, high):
    def one(dim, shards_of):
        steps = jax.random.uniform(jax.random.fold_in(jax.random.fold_in(own_key, 6), dim), (shards_of,), jnp.float32, low / len(cuts), high / len(cuts))
        return jnp.repeat(jnp.exp(steps), extent[dim] // shards_of).reshape((-1,) + (1,) * (len(extent) - dim - 1))

    loudness = one(*cuts[0])
    for cut in cuts[1:]:
        loudness = loudness * one(*cut)
    return loudness


def normal_values(own_key, dims, deviation, bound, shards=(), kind=jnp.bfloat16):
    entries = jax.random.normal(own_key, dims, jnp.float32) * deviation
    if len(shards) > 0:
        entries = block_levels(own_key, dims, shards, -0.22, 0.18) * entries
    return jnp.clip(entries, min=-bound, max=bound).astype(kind)


def setup_inputs(seed: int = 0) -> dict:
    key_list = jax.random.split(jax.random.key(seed), 4)
    activations = normal_values(key_list[0], (CLIENTS, SLOTS, HH, IMG_W, CH), 1.0, 6.0, ((0, 4), (2, 8)))
    sample_count = draw_sample_count(jax.random.fold_in(key_list[3], 71), 0)
    client_weights = normal_values(key_list[2], (CLIENTS, KK, COUT), 1.0, 6.0, ((0, 4), (1, 8)))
    return {"activations": activations, "sample_count": sample_count, "client_weights": client_weights}


keep_off = 0.9


def patch_rows(images):
    groups, slots, img_height, img_width, channel_count = images.shape
    padded = jnp.pad(images, [(0, 0), (0, 0), (1, 1), (1, 1), (0, 0)])
    shifted = [padded[:, :, row_off:row_off + img_height, col_off:col_off + img_width, :] for row_off in range(3) for col_off in range(3)]
    stacked = jnp.stack(shifted, axis=-1)
    return stacked.reshape(groups, slots * img_height * img_width, channel_count * 9)


def reference(activations, sample_count, client_weights):
    live = lax.broadcasted_iota(jnp.int32, (CLIENTS, SLOTS), 1) < sample_count[:, None]
    masked = jnp.where(live[:, :, None, None, None], activations, jnp.zeros_like(activations))
    patches = patch_rows(masked)
    scales = 1.0 / (CLIENTS * sample_count.astype(jnp.float32) * (HH * IMG_W))

    def accumulate(running, inputs):
        patch_one, scale_one, weight_one = inputs
        gram_part = jnp.dot(patch_one.T, patch_one, preferred_element_type=jnp.float32)
        outputs = jnp.dot(patch_one, weight_one, preferred_element_type=jnp.float32).astype(jnp.bfloat16)
        cross = jnp.dot(patch_one.T, outputs, preferred_element_type=jnp.float32)
        diag_part = jnp.sum(jnp.square(patch_one.astype(jnp.float32)), axis=0)
        rhs_part = keep_off * cross + (1.0 - keep_off) * diag_part[:, None] * weight_one.astype(jnp.float32)
        return (running[0] + scale_one * gram_part, running[1] + scale_one * rhs_part), None

    start_state = (jnp.zeros((KK, KK), jnp.float32), jnp.zeros((KK, COUT), jnp.float32))
    (summed, merged_rhs), _ = lax.scan(accumulate, start_state, (patches, scales, client_weights))
    on_diag = lax.broadcasted_iota(jnp.int32, (KK, KK), 0) == lax.broadcasted_iota(jnp.int32, (KK, KK), 1)
    merged_gram = jnp.where(on_diag, summed, keep_off * summed)
    return merged_gram, merged_rhs
```

```python
import functools

import jax
import jax.numpy as jnp
from jax import lax
from jax.experimental import pallas as pl
from jax.experimental.pallas import tpu as pltpu
from jax.sharding import PartitionSpec as P

keep_off = 0.9
LANES = 128
KCHUNKS = 8


MESH = pl.DeviceIdType.MESH


def expand(base_of, live, channels, scratch, height, stride, width):
    pixels = live.shape[1]
    lane = lax.broadcasted_iota(jnp.int32, (1, pixels), 1)
    col = lane % width
    row = (lane // stride) % height

    def shifted(value, step, inside):
        return jnp.where(inside, pltpu.roll(value, (-step) % pixels, 1), 0.0)

    for first in range(0, channels, 16):
        size = min(16, channels - first)
        base = jnp.where(live > 0.0, base_of(first, size), 0.0)
        for b in range(3):
            if b == 1:
                across = base
            else:
                across = shifted(base, b - 1, (col + (b - 1) >= 0) & (col + (b - 1) < width))
            for a in range(3):
                if a == 1:
                    both = across
                else:
                    both = shifted(across, (a - 1) * stride, (row + (a - 1) >= 0) & (row + (a - 1) < height))
                for chunk in range(pixels // LANES):
                    scratch[chunk, pl.ds(first * 9 + 3 * a + b, size, stride=9), :] = both[
                        :, chunk * LANES : (chunk + 1) * LANES
                    ]


def spread(rows_of, live, channels, scratch, chunks, first_chunk, width):
    col = lax.broadcasted_iota(jnp.int32, (1, LANES), 1) % width
    held = scratch.shape[0]
    for h in range(max(first_chunk - 1, 0), min(first_chunk + held + 1, chunks)):
        value = rows_of(h)
        for first in range(0, channels, 8):
            size = min(8, channels - first)
            base = jnp.where(live > 0.0, value[first : first + size], 0.0)
            for b in range(3):
                if b == 1:
                    across = base
                else:
                    inside = (col + (b - 1) >= 0) & (col + (b - 1) < width)
                    across = jnp.where(inside, pltpu.roll(base, (1 - b) % LANES, 1), 0.0)
                for a in range(3):
                    to = h + 1 - a - first_chunk
                    if 0 <= to < held:
                        scratch[to, pl.ds(first * 9 + 3 * a + b, size, stride=9), :] = across
    for edge, a in ((0, 0), (chunks - 1, 2)):
        to = edge - first_chunk
        if 0 <= to < held:
            for first in range(0, channels, 8):
                size = min(8, channels - first)
                for b in range(3):
                    scratch[to, pl.ds(first * 9 + 3 * a + b, size, stride=9), :] = jnp.zeros(
                        (size, LANES), jnp.float32
                    )


def client_lanes(count_ref, first, clients, client, slot, total):
    count = jnp.zeros(client.shape, jnp.int32)
    for index in range(clients):
        count = jnp.where(client == index, count_ref[first + index], count)
    live = jnp.where(slot < count, 1.0, 0.0)
    return live, 1.0 / (total * count.astype(jnp.float32))


def step_kernel(
    groups, slots, width, count_ref, x_ref, w_ref, gram_ref, rhs_ref,
    xall, tsend, trecv, flat, wbuf, tall_wide, patch, scaled, across, square,
    part_ref, ybuf, sums, zbuf, obuf, rbuf, abuf, cbuf, vbuf, ubuf, wide, narrow, mine_ref,
    tss, tsr, hs, hr, ws, ys, yr, zs, zr, gs, gr, fs, fr, cs, cr, vs, vr,
):
    blks, clients, stride, channels = xall.shape
    height = blks
    pieces, depth = part_ref.shape[:2]
    cols = part_ref.shape[4]
    tile = trecv.shape[2]
    tall = tall_wide.shape[1]
    pixels = height * stride
    image = slots * width
    mine = rhs_ref.shape[0]
    total = count_ref.shape[0] * height * width
    client, blk = lax.axis_index("client"), lax.axis_index("blk")
    z, y = blk // 2, blk % 2
    core, side = client % 2, client // 2
    other = 1 - y
    core_mate = client + 1 - 2 * core
    x_mate = (client + 2) % clients
    core_dev, x_dev, y_dev = (core_mate, blk), (x_mate, blk), (client, blk + 1 - 2 * y)
    up_dev, down_dev = (client, blk + 2), (client, blk - 2)

    def level(d):
        return (z + d) % depth

    def z_dev(d):
        return (client, level(d) * 2 + y)

    def near(d):
        return (blk + d) % blks

    def w_copy(q):
        return pltpu.make_async_copy(w_ref.at[:, :, pl.ds(q * cols, cols)], wbuf.at[q], ws.at[q])

    for q in range(pieces):
        w_copy(q).start()

    barrier = pltpu.get_barrier_semaphore()
    for device in [core_dev, x_dev] + [(client, near(d)) for d in range(1, blks)]:
        pl.semaphore_signal(barrier, inc=1, device_id=device, device_id_type=MESH)
    for b in range(blks):
        tsend[b] = x_ref[:, b * tile : (b + 1) * tile]
    xall[blk, client] = x_ref[...]
    pl.semaphore_wait(barrier, blks + 1)

    def send(src, dst, send_sem, recv_sem, device):
        return pltpu.make_async_remote_copy(
            src_ref=src, dst_ref=dst, send_sem=send_sem, recv_sem=recv_sem, device_id=device, device_id_type=MESH
        )

    def tile_copy(d):
        return send(tsend.at[near(d)], trecv.at[blk], tss.at[d], tsr.at[blk], (client, near(d)))

    def tile_arrival(d):
        here = trecv.at[near(d)]
        return send(here, here, tss.at[d], tsr.at[near(d)], (client, near(d)))

    def hop(lane, c, b, device, own=False):
        dst = xall.at[b, c]
        src = x_ref if own else dst
        return send(src, dst, hs.at[lane, c * blks + b], hr.at[c * blks + b], device)

    def relay(d, mate, act, arrive=True):
        own = d == 0 and not mate

        def forward_block():
            b = (z + d) * 2 + (other if mate else y)
            if arrive and not own:
                hop(0, client, b, core_dev).wait_recv()
            if own:
                act(hop(3, client, b, y_dev, own))
            if d <= 0:
                pl.when(z + 1 < depth)(lambda: act(hop(0, client, b, up_dev, own)))
            if d >= 0:
                pl.when(z > 0)(lambda: act(hop(1, client, b, down_dev, own)))
            act(hop(2, client, b, x_dev, own))
            act(hop(4, client, b, core_dev, own))

        if d == 0:
            forward_block()
        else:
            pl.when((z + d >= 0) & (z + d < depth))(forward_block)

    def hand_over(b, act, arrive=True):
        if arrive:
            hop(2, x_mate, b, core_dev).wait_recv()
        act(hop(4, x_mate, b, core_dev))

    def start(copy):
        copy.start()

    def wait_send(copy):
        copy.wait_send()

    line = [(0, False), (0, True)]
    for distance in range(1, depth):
        line += [(-distance, False), (distance, False), (-distance, True), (distance, True)]

    for d in range(1, blks):
        tile_copy(d).start()
    relay(0, False, start)

    def y_copy(q):
        return send(part_ref.at[q, :, other], ybuf.at[q], ys.at[q], yr.at[q], y_dev)

    def z_copy(q, d):
        return send(sums.at[q, level(d)], zbuf.at[q, d], zs.at[q, d], zr.at[q, d], z_dev(d))

    def share(q, d, to):
        here = obuf.at[q, level(d), y]
        return send(here, here, gs.at[q, to], gr.at[q, to], z_dev(to))

    def forward(q, d, column):
        here = obuf.at[q, level(d), column]
        return send(here, here, fs.at[q, d], fr.at[q, level(d)], y_dev)

    def core_copy(q):
        return send(abuf.at[q], cbuf.at[q], cs.at[q], cr.at[q], core_dev)

    def x_copy(q):
        return send(vbuf.at[q], ubuf.at[q], vs.at[q], vr.at[q], x_dev)

    lane = lax.broadcasted_iota(jnp.int32, (1, pixels), 1)
    who = (lane // image) % groups
    live, scale = client_lanes(count_ref, client * groups, groups, who, (lane // width) % slots, total)

    def patches():
        trecv[blk] = tsend[blk]
        for d in range(1, blks):
            tile_arrival(d).wait_recv()
        flat[...] = trecv[...].reshape(pixels, tile).astype(jnp.float32).T
        expand(lambda first, size: flat[first : first + size, :], live, tile, tall_wide, height, stride, width)
        for chunk in range(tall_wide.shape[0]):
            span = slice(chunk * LANES, (chunk + 1) * LANES)
            value = tall_wide[chunk]
            patch[:, span] = value.astype(jnp.bfloat16)
            scaled[:, span] = (value * scale[:, span]).astype(jnp.bfloat16)
        flipped = patch[...].T
        for h in range(height):
            for group in range(groups):
                across[group, h * image : (h + 1) * image] = flipped[
                    (h * groups + group) * image : (h * groups + group + 1) * image
                ]

    def multiply(q):
        w_copy(q).wait()
        for group in range(groups):
            term = jnp.dot(across[group], wbuf[q, group], preferred_element_type=jnp.float32)
            for h in range(height):
                part_ref[q, h // 2, h % 2, group * image : (group + 1) * image] = term[h * image : (h + 1) * image]
        y_copy(q).start()

    def damping():
        for group in range(groups):
            term = jnp.zeros((tall, 1), jnp.float32)
            for chunk in range(tall_wide.shape[0]):
                span = slice(chunk * LANES, (chunk + 1) * LANES)
                value = tall_wide[chunk]
                value = jnp.where(who[:, span] == group, value * value * scale[:, span], 0.0)
                term += jnp.sum(value, axis=1, keepdims=True)
            square[group] = term * (1.0 - keep_off)

    def damp(q):
        total = None
        for group in range(groups):
            term = square[group] * wbuf[q, group].astype(jnp.float32)
            total = term if total is None else total + term
        rbuf[q] = total

    def add_y(q):
        y_copy(q).wait_recv()
        for d in range(depth):
            sums[q, level(d)] = part_ref[q, level(d), y] + ybuf[q, level(d)]
        for d in range(1, depth):
            z_copy(q, d).start()

    def add_z(q):
        total = sums[q, z]
        for d in range(1, depth):
            z_copy(q, d).wait_recv()
            total = total + zbuf[q, d]
        obuf[q, z, y] = total.astype(jnp.bfloat16)
        for d in range(1, depth):
            share(q, 0, d).start()
        forward(q, 0, y).start()

    def pass_on(q):
        for d in range(1, depth):
            share(q, depth - d, d).wait_recv()
            forward(q, depth - d, y).start()

    def rows_of(q, holder):
        if mine % 8 == 0:
            return rbuf[q, pl.ds(pl.multiple_of(holder * mine, 8), mine), :]
        value = rbuf[q, :mine, :]
        for index in range(1, tall // mine):
            value = jnp.where(holder == index, rbuf[q, index * mine : (index + 1) * mine, :], value)
        return value

    def cross(q):
        for d in range(depth):
            forward(q, d, other).wait_recv()
        product = jnp.dot(scaled[...], obuf[q].reshape(pixels, cols), preferred_element_type=jnp.float32)
        rbuf[q] = rbuf[q] + keep_off * product
        for far in range(2):
            abuf[q, far] = rows_of(q, far * 2 + 1 - core).astype(jnp.bfloat16)
        core_copy(q).start()

    def finish(q):
        core_copy(q).wait_recv()
        far = 1 - side
        away = rows_of(q, far * 2 + core) + cbuf[q, far].astype(jnp.float32)
        vbuf[q] = away.astype(jnp.bfloat16)
        x_copy(q).start()
        span = slice(q * cols, (q + 1) * cols)
        rhs_ref[:, span] = rows_of(q, client) + cbuf[q, side].astype(jnp.float32)

    def settle(q):
        x_copy(q).wait_recv()
        span = slice(q * cols, (q + 1) * cols)
        rhs_ref[:, span] = rhs_ref[:, span] + ubuf[q].astype(jnp.float32)

    def tick(step):
        if step < pieces:
            add_y(step)
        if 0 <= step - 1 < pieces:
            add_z(step - 1)
        if step < pieces:
            damp(step)
        if 0 <= step - 2 < pieces:
            pass_on(step - 2)
        if 0 <= step - 3 < pieces:
            cross(step - 3)
        if 0 <= step - 4 < pieces:
            finish(step - 4)

    patches()
    later = line[1:]
    for q in range(pieces):
        for entry in later[:2]:
            relay(*entry, start)
        later = later[2:]
        multiply(q)
    damping()
    for entry in later:
        relay(*entry, start)
    crossing = [(z + d) % depth * 2 + p for d in range(depth) for p in (0, 1)]
    before = 3
    each = -(-len(crossing) // before)
    for step in range(before):
        tick(step)
        for b in crossing[step * each : (step + 1) * each]:
            hand_over(b, start)
    far_mate = (core_mate + 2) % clients
    for b in range(blks):
        for c in (core_mate, far_mate):
            hop(4, c, b, core_dev).wait_recv()

    own = blk * tile + client * (mine // 9)
    span = lax.broadcasted_iota(jnp.int32, (1, LANES), 1)
    all_live, all_scale = client_lanes(
        count_ref, 0, count_ref.shape[0], span // image, (span // width) % slots, total
    )
    held = wide.shape[0]
    passes = [first for first in range(0, height, held)]

    def block_rows(h, lanes):
        return xall[h, :, :, lanes].reshape(LANES, -1)

    chosen = (
        lax.broadcasted_iota(jnp.int32, (mine // 9, channels), 1)
        == lax.broadcasted_iota(jnp.int32, (mine // 9, channels), 0) + own
    )
    chosen = jnp.where(chosen, 1.0, 0.0).astype(jnp.bfloat16)

    def own_rows(h):
        return lax.dot_general(
            chosen, block_rows(h, slice(None)), (((1,), (1,)), ((), ())), preferred_element_type=jnp.float32
        )

    for first in passes:
        spread(own_rows, all_live, mine // 9, wide, height, first, width)
        for chunk in range(held):
            mine_ref[:, (first + chunk) * LANES : (first + chunk + 1) * LANES] = (
                wide[chunk, :mine] * all_scale
            ).astype(jnp.bfloat16)

    tiles = gram_ref.shape[0]
    events = {}
    for index, step in enumerate(range(before, pieces + 4)):
        events.setdefault(min(index, tiles - 1), []).append(functools.partial(tick, step))

    def gram_tile(t, carry):
        for when, actions in events.items():

            @pl.when(t == when)
            def _():
                for action in actions:
                    action()

        lanes = pl.ds(pl.multiple_of(t * LANES, LANES), LANES)
        for first in passes:
            spread(
                lambda h: block_rows(h, lanes).astype(jnp.float32).T, all_live, LANES, wide, height, first, width
            )
            for chunk in range(held):
                narrow[:, chunk * LANES : (chunk + 1) * LANES] = wide[chunk].astype(jnp.bfloat16)
            product = lax.dot_general(
                mine_ref[:, first * LANES : (first + held) * LANES], narrow[...],
                (((1,), (1,)), ((), ())), preferred_element_type=jnp.float32,
            )
            if first != 0:
                product = product + gram_ref[t]
            if first == passes[-1]:
                where_diag = own * 9 - t * product.shape[1]
                on_diag = (
                    lax.broadcasted_iota(jnp.int32, product.shape, 1)
                    == lax.broadcasted_iota(jnp.int32, product.shape, 0) + where_diag
                )
                product = jnp.where(on_diag, product, keep_off * product)
            gram_ref[t] = product
        return carry

    lax.fori_loop(0, tiles, gram_tile, 0)

    for q in range(pieces):
        settle(q)
    for entry in line:
        relay(*entry, wait_send, False)
    for b in crossing:
        hand_over(b, wait_send, False)
    for d in range(1, blks):
        tile_copy(d).wait_send()
    for q in range(pieces):
        y_copy(q).wait_send()
        core_copy(q).wait_send()
        x_copy(q).wait_send()
        for d in range(1, depth):
            z_copy(q, d).wait_send()
            share(q, 0, d).wait_send()
        for d in range(depth):
            forward(q, d, y).wait_send()


def step_call(counts, x, weights, clients, blks, slots, width):
    stride, channels = x.shape
    groups, tall, columns = weights.shape
    mine = tall // clients
    tile = tall // 9
    height = blks
    pixels = height * stride
    everyone = clients * stride
    pieces = columns // 256 if columns % 256 == 0 else 1
    cols = columns // pieces
    depth = blks // 2
    held = min(KCHUNKS, height)
    sem = pltpu.SemaphoreType.DMA
    f32, bf16 = jnp.float32, jnp.bfloat16
    hop = pltpu.VMEM((pieces, depth, stride, cols), f32)
    return pl.pallas_call(
        functools.partial(step_kernel, groups, slots, width),
        in_specs=[
            pl.BlockSpec(memory_space=pltpu.SMEM),
            pl.BlockSpec(memory_space=pltpu.VMEM),
            pl.BlockSpec(memory_space=pltpu.HBM),
        ],
        out_specs=[pl.BlockSpec(memory_space=pltpu.VMEM)] * 2,
        out_shape=[
            pltpu.VMEM((channels // LANES, mine, LANES * 9), f32),
            pltpu.VMEM((mine, columns), f32),
        ],
        scratch_shapes=[
            pltpu.VMEM((blks, clients, stride, channels), bf16),
            pltpu.VMEM((blks, stride, tile), bf16),
            pltpu.VMEM((blks, stride, tile), bf16),
            pltpu.VMEM((tile, pixels), f32),
            pltpu.VMEM((pieces, groups, tall, cols), bf16),
            pltpu.VMEM((pixels // LANES, tall, LANES), f32),
            pltpu.VMEM((tall, pixels), bf16),
            pltpu.VMEM((tall, pixels), bf16),
            pltpu.VMEM((groups, pixels // groups, tall), bf16),
            pltpu.VMEM((groups, tall, 1), f32),
            pltpu.VMEM((pieces, depth, 2, stride, cols), f32),
            hop,
            hop,
            hop,
            pltpu.VMEM((pieces, depth, 2, stride, cols), bf16),
            pltpu.VMEM((pieces, tall, cols), f32),
            pltpu.VMEM((pieces, 2, mine, cols), bf16),
            pltpu.VMEM((pieces, 2, mine, cols), bf16),
            pltpu.VMEM((pieces, mine, cols), bf16),
            pltpu.VMEM((pieces, mine, cols), bf16),
            pltpu.VMEM((held, LANES * 9, LANES), f32),
            pltpu.VMEM((LANES * 9, held * LANES), bf16),
            pltpu.VMEM((mine, height * LANES), bf16),
            sem((blks,)),
            sem((blks,)),
            sem((5, clients * blks)),
            sem((clients * blks,)),
            sem((pieces,)),
            sem((pieces,)),
            sem((pieces,)),
        ]
        + [sem((pieces, depth))] * 6
        + [sem((pieces,))] * 4,
        compiler_params=pltpu.CompilerParams(
            collective_id=1, has_side_effects=True, vmem_limit_bytes=VMEM_MIB * 1024 * 1024
        ),
    )(counts, x, weights)


VMEM_MIB = 44


def store_kernel(gram_tiles, rhs_ref, gram_ref, out_ref, sems):
    tiles, rows, wide = gram_tiles.shape

    def tile_copy(t):
        return pltpu.make_async_copy(gram_tiles.at[t], gram_ref.at[:, pl.ds(t * wide, wide)], sems.at[t])

    rhs_copy = pltpu.make_async_copy(rhs_ref, out_ref, sems.at[tiles])
    for t in range(tiles):
        tile_copy(t).start()
    rhs_copy.start()
    for t in range(tiles):
        tile_copy(t).wait()
    rhs_copy.wait()


def store_call(gram_tiles, rhs):
    tiles, rows, wide = gram_tiles.shape
    return pl.pallas_call(
        store_kernel,
        in_specs=[pl.BlockSpec(memory_space=pltpu.VMEM)] * 2,
        out_specs=[pl.BlockSpec(memory_space=pl.ANY)] * 2,
        out_shape=[
            jax.ShapeDtypeStruct((rows, tiles * wide), jnp.float32),
            jax.ShapeDtypeStruct(rhs.shape, jnp.float32),
        ],
        scratch_shapes=[pltpu.SemaphoreType.DMA((tiles + 1,))],
        compiler_params=pltpu.CompilerParams(vmem_limit_bytes=24 * 1024 * 1024),
    )(gram_tiles, rhs)


def body(activations, sample_count, client_weights):
    blk_count = lax.axis_size("blk")
    group_size, slot_count, rows_here, width, channels = activations.shape
    client_groups = sample_count.shape[0] // group_size
    assert rows_here == 1 and client_groups * group_size * slot_count * width == LANES
    shard = activations.transpose(2, 0, 1, 3, 4).reshape(group_size * slot_count * width, channels)
    gram_tiles, rhs = step_call(
        sample_count, shard, client_weights, client_groups, blk_count, slot_count, width
    )
    return tuple(store_call(gram_tiles, rhs))


def solution(mesh):
    in_specs = (P("client", None, "blk", None, None), P(), P("client", "blk", None))
    out_specs = (P(("blk", "client"), None), P(("blk", "client"), None))
    return jax.shard_map(body, mesh=mesh, in_specs=in_specs, out_specs=out_specs, check_vma=False)
```

```python
import functools

import jax
import jax.numpy as jnp
from jax import lax
from jax.experimental import pallas as pl
from jax.experimental.pallas import tpu as pltpu
from jax.sharding import PartitionSpec as P

keep_off = 0.9
LANES = 128
KCHUNKS = 8


MESH = pl.DeviceIdType.MESH


def expand(base_of, live, channels, scratch, height, stride, width):
    pixels = live.shape[1]
    lane = lax.broadcasted_iota(jnp.int32, (1, pixels), 1)
    col = lane % width
    row = (lane // stride) % height

    def shifted(value, step, inside):
        return jnp.where(inside, pltpu.roll(value, (-step) % pixels, 1), 0.0)

    for first in range(0, channels, 16):
        size = min(16, channels - first)
        base = jnp.where(live > 0.0, base_of(first, size), 0.0)
        for b in range(3):
            if b == 1:
                across = base
            else:
                across = shifted(base, b - 1, (col + (b - 1) >= 0) & (col + (b - 1) < width))
            for a in range(3):
                if a == 1:
                    both = across
                else:
                    both = shifted(across, (a - 1) * stride, (row + (a - 1) >= 0) & (row + (a - 1) < height))
                for chunk in range(pixels // LANES):
                    scratch[chunk, pl.ds(first * 9 + 3 * a + b, size, stride=9), :] = both[
                        :, chunk * LANES : (chunk + 1) * LANES
                    ]


def spread(rows_of, live, channels, scratch, chunks, first_chunk, width):
    col = lax.broadcasted_iota(jnp.int32, (1, LANES), 1) % width
    held = scratch.shape[0]
    for h in range(max(first_chunk - 1, 0), min(first_chunk + held + 1, chunks)):
        value = rows_of(h)
        for first in range(0, channels, 8):
            size = min(8, channels - first)
            base = jnp.where(live > 0.0, value[first : first + size], 0.0)
            for b in range(3):
                if b == 1:
                    across = base
                else:
                    inside = (col + (b - 1) >= 0) & (col + (b - 1) < width)
                    across = jnp.where(inside, pltpu.roll(base, (1 - b) % LANES, 1), 0.0)
                for a in range(3):
                    to = h + 1 - a - first_chunk
                    if 0 <= to < held:
                        scratch[to, pl.ds(first * 9 + 3 * a + b, size, stride=9), :] = across
    for edge, a in ((0, 0), (chunks - 1, 2)):
        to = edge - first_chunk
        if 0 <= to < held:
            for first in range(0, channels, 8):
                size = min(8, channels - first)
                for b in range(3):
                    scratch[to, pl.ds(first * 9 + 3 * a + b, size, stride=9), :] = jnp.zeros(
                        (size, LANES), jnp.float32
                    )


START, GRAM, TILE, OVER = 12.5, 27.0, 1.9, 1.1
PIECE = 256


def plan(pieces, depth, part, tiles):
    listed = [(START + 0.46 * part * pieces, "damping")]
    for q in range(pieces):
        at = START + 0.45 * part * q
        listed.append((at, "multiply", q))
        listed.append((START + 0.47 * part * pieces + 0.5 * part * q, "damp", q))
        at = START + 1.5 + 2.8 * part * (q + 1)
        listed.append((at, "add_y", q))
        for name, wait in (
            ("add_z", 2.8 * part + 2.5), ("pass_on", 1.4 * part + 2.5),
            ("cross", 1.4 * part + 1.5), ("finish", 0.8 * part + 1.7),
        ):
            at += wait
            listed.append((at, name, q))
    for index in range(4 * depth - 2):
        distance = (index + 2) // 4
        at = START - 1.0 + 2.2 * (distance - 1) + 1.5 * (index % 4 in (0, 1) if distance else index)
        if index > 3:
            listed.append((at, "relay", index))
        listed.append((max(at + 3.0, START - 0.5 + OVER * index), "over", index))
    listed.sort(key=lambda entry: entry[0])
    before = [entry[1:] for entry in listed if entry[0] < GRAM or entry[1] in ("relay", "over")]
    during = [[] for _ in range(tiles + 1)]
    for at, *entry in listed:
        if tuple(entry) not in before:
            during[min(int((at - GRAM) / TILE), tiles)].append(tuple(entry))
    return before, during


def client_lanes(count_ref, first, clients, client, slot, total):
    count = jnp.zeros(client.shape, jnp.int32)
    for index in range(clients):
        count = jnp.where(client == index, count_ref[first + index], count)
    live = jnp.where(slot < count, 1.0, 0.0)
    return live, 1.0 / (total * count.astype(jnp.float32))


def step_kernel(
    groups, slots, width, count_ref, x_ref, w_ref, gram_ref, rhs_ref,
    xall, tsend, trecv, flat, wbuf, tall_wide, patch, scaled, across, square,
    part_ref, ybuf, sums, zbuf, obuf, rbuf, abuf, cbuf, vbuf, ubuf, wide, narrow, narrow_next, mine_ref,
    tss, tsr, hs, hr, ws, ys, yr, zs, zr, gs, gr, fs, fr, cs, cr, vs, vr,
):
    blks, clients, stride, channels = xall.shape
    height = blks
    pieces, depth = part_ref.shape[:2]
    cols = part_ref.shape[4]
    tile = trecv.shape[2]
    tall = tall_wide.shape[1]
    pixels = height * stride
    image = slots * width
    mine = rhs_ref.shape[0]
    total = count_ref.shape[0] * height * width
    client, blk = lax.axis_index("client"), lax.axis_index("blk")
    z, y = blk // 2, blk % 2
    core, side = client % 2, client // 2
    other = 1 - y
    core_mate = client + 1 - 2 * core
    x_mate = (client + 2) % clients
    core_dev, x_dev, y_dev = (core_mate, blk), (x_mate, blk), (client, blk + 1 - 2 * y)
    up_dev, down_dev = (client, blk + 2), (client, blk - 2)

    def level(d):
        return (z + d) % depth

    def z_dev(d):
        return (client, level(d) * 2 + y)

    def near(d):
        return (blk + d) % blks

    def w_copy(q):
        return pltpu.make_async_copy(w_ref.at[:, :, pl.ds(q * cols, cols)], wbuf.at[q], ws.at[q])

    for q in range(pieces):
        w_copy(q).start()

    barrier = pltpu.get_barrier_semaphore()
    for device in [core_dev, x_dev] + [(client, near(d)) for d in range(1, blks)]:
        pl.semaphore_signal(barrier, inc=1, device_id=device, device_id_type=MESH)
    for b in range(blks):
        tsend[b] = x_ref[:, b * tile : (b + 1) * tile]
    xall[blk, client] = x_ref[...]
    pl.semaphore_wait(barrier, blks + 1)

    def send(src, dst, send_sem, recv_sem, device):
        return pltpu.make_async_remote_copy(
            src_ref=src, dst_ref=dst, send_sem=send_sem, recv_sem=recv_sem, device_id=device, device_id_type=MESH
        )

    def tile_copy(d):
        return send(tsend.at[near(d)], trecv.at[blk], tss.at[d], tsr.at[blk], (client, near(d)))

    def tile_arrival(d):
        here = trecv.at[near(d)]
        return send(here, here, tss.at[d], tsr.at[near(d)], (client, near(d)))

    def hop(lane, c, b, device, own=False):
        dst = xall.at[b, c]
        src = x_ref if own else dst
        return send(src, dst, hs.at[lane, c * blks + b], hr.at[c * blks + b], device)

    def relay(d, mate, act, arrive=True):
        own = d == 0 and not mate

        def forward_block():
            b = (z + d) * 2 + (other if mate else y)
            if arrive and not own:
                hop(0, client, b, core_dev).wait_recv()
            if own:
                act(hop(3, client, b, y_dev, own))
            if d <= 0:
                pl.when(z + 1 < depth)(lambda: act(hop(0, client, b, up_dev, own)))
            if d >= 0:
                pl.when(z > 0)(lambda: act(hop(1, client, b, down_dev, own)))
            act(hop(2, client, b, x_dev, own))
            act(hop(4, client, b, core_dev, own))

        if d == 0:
            forward_block()
        else:
            pl.when((z + d >= 0) & (z + d < depth))(forward_block)

    def hand_over(d, mate, act, arrive=True):
        def pass_block():
            b = (z + d) * 2 + (other if mate else y)
            if arrive:
                hop(2, x_mate, b, core_dev).wait_recv()
            act(hop(4, x_mate, b, core_dev))

        if d == 0:
            pass_block()
        else:
            pl.when((z + d >= 0) & (z + d < depth))(pass_block)

    def start(copy):
        copy.start()

    def wait_send(copy):
        copy.wait_send()

    line = [(0, False), (0, True)]
    for distance in range(1, depth):
        line += [(-distance, False), (distance, False), (-distance, True), (distance, True)]

    for d in range(1, blks):
        tile_copy(d).start()
    relay(0, False, start)

    def y_copy(q):
        return send(part_ref.at[q, :, other], ybuf.at[q], ys.at[q], yr.at[q], y_dev)

    def z_copy(q, d):
        return send(sums.at[q, level(d)], zbuf.at[q, d], zs.at[q, d], zr.at[q, d], z_dev(d))

    def share(q, d, to):
        here = obuf.at[q, level(d), y]
        return send(here, here, gs.at[q, to], gr.at[q, to], z_dev(to))

    def forward(q, d, column):
        here = obuf.at[q, level(d), column]
        return send(here, here, fs.at[q, d], fr.at[q, level(d)], y_dev)

    def core_copy(q):
        return send(abuf.at[q], cbuf.at[q], cs.at[q], cr.at[q], core_dev)

    def x_copy(q):
        return send(vbuf.at[q], ubuf.at[q], vs.at[q], vr.at[q], x_dev)

    lane = lax.broadcasted_iota(jnp.int32, (1, pixels), 1)
    who = (lane // image) % groups
    live, scale = client_lanes(count_ref, client * groups, groups, who, (lane // width) % slots, total)

    def patches():
        trecv[blk] = tsend[blk]
        for d in range(1, blks):
            tile_arrival(d).wait_recv()
        for index in range(1, 4):
            relay(*line[index], start)
        flat[...] = trecv[...].reshape(pixels, tile).astype(jnp.float32).T
        expand(lambda first, size: flat[first : first + size, :], live, tile, tall_wide, height, stride, width)
        for chunk in range(tall_wide.shape[0]):
            span = slice(chunk * LANES, (chunk + 1) * LANES)
            value = tall_wide[chunk]
            patch[:, span] = value.astype(jnp.bfloat16)
            scaled[:, span] = (value * scale[:, span]).astype(jnp.bfloat16)
        flipped = patch[...].T
        for h in range(height):
            for group in range(groups):
                across[group, h * image : (h + 1) * image] = flipped[
                    (h * groups + group) * image : (h * groups + group + 1) * image
                ]

    def multiply(q):
        w_copy(q).wait()
        for group in range(groups):
            term = jnp.dot(across[group], wbuf[q, group], preferred_element_type=jnp.float32)
            for h in range(height):
                part_ref[q, h // 2, h % 2, group * image : (group + 1) * image] = term[h * image : (h + 1) * image]
        y_copy(q).start()

    def damping():
        for group in range(groups):
            term = jnp.zeros((tall, 1), jnp.float32)
            for chunk in range(tall_wide.shape[0]):
                span = slice(chunk * LANES, (chunk + 1) * LANES)
                value = tall_wide[chunk]
                value = jnp.where(who[:, span] == group, value * value * scale[:, span], 0.0)
                term += jnp.sum(value, axis=1, keepdims=True)
            square[group] = jnp.broadcast_to(term * (1.0 - keep_off), (tall, LANES))

    def damp(q):
        rows = 80 if tall % 80 == 0 else tall

        def block(index, carry):
            span = pl.ds(pl.multiple_of(index * rows, 8), rows)
            for first in range(0, cols, LANES):
                total = None
                for group in range(groups):
                    term = square[group, span, :] * wbuf[q, group, span, first : first + LANES].astype(jnp.float32)
                    total = term if total is None else total + term
                rbuf[q, span, first : first + LANES] = total
            return carry

        lax.fori_loop(0, tall // rows, block, 0)

    def add_y(q):
        y_copy(q).wait_recv()
        for d in range(depth):
            sums[q, level(d)] = part_ref[q, level(d), y] + ybuf[q, level(d)]
        for d in range(1, depth):
            z_copy(q, d).start()

    def add_z(q):
        total = sums[q, z]
        for d in range(1, depth):
            z_copy(q, d).wait_recv()
            total = total + zbuf[q, d]
        obuf[q, z, y] = total.astype(jnp.bfloat16)
        for d in range(1, depth):
            share(q, 0, d).start()
        forward(q, 0, y).start()

    def pass_on(q):
        for d in range(1, depth):
            share(q, depth - d, d).wait_recv()
            forward(q, depth - d, y).start()

    def rows_of(q, holder):
        if mine % 8 == 0:
            return rbuf[q, pl.ds(pl.multiple_of(holder * mine, 8), mine), :]
        value = rbuf[q, :mine, :]
        for index in range(1, tall // mine):
            value = jnp.where(holder == index, rbuf[q, index * mine : (index + 1) * mine, :], value)
        return value

    def cross(q):
        for d in range(depth):
            forward(q, d, other).wait_recv()
        product = jnp.dot(scaled[...], obuf[q].reshape(pixels, cols), preferred_element_type=jnp.float32)
        rbuf[q] = rbuf[q] + keep_off * product
        for far in range(2):
            abuf[q, far] = rows_of(q, far * 2 + 1 - core).astype(jnp.bfloat16)
        core_copy(q).start()

    def finish(q):
        core_copy(q).wait_recv()
        far = 1 - side
        away = rows_of(q, far * 2 + core) + cbuf[q, far].astype(jnp.float32)
        vbuf[q] = away.astype(jnp.bfloat16)
        x_copy(q).start()
        span = slice(q * cols, (q + 1) * cols)
        rhs_ref[:, span] = rows_of(q, client) + cbuf[q, side].astype(jnp.float32)

    def settle(q):
        x_copy(q).wait_recv()
        span = slice(q * cols, (q + 1) * cols)
        rhs_ref[:, span] = rhs_ref[:, span] + ubuf[q].astype(jnp.float32)

    actions = {
        "multiply": multiply,
        "damping": damping,
        "damp": damp,
        "add_y": add_y,
        "add_z": add_z,
        "pass_on": pass_on,
        "cross": cross,
        "finish": finish,
        "relay": lambda index: relay(*line[index], start),
        "over": lambda index: hand_over(*line[index], start),
    }

    def run(listed):
        for name, *values in listed:
            actions[name](*values)

    before, during = plan(pieces, depth, cols / 256, gram_ref.shape[0])
    patches()
    run(before)
    far_mate = (core_mate + 2) % clients
    for b in range(blks):
        for c in (core_mate, far_mate):
            hop(4, c, b, core_dev).wait_recv()

    own = blk * tile + client * (mine // 9)
    span = lax.broadcasted_iota(jnp.int32, (1, LANES), 1)
    all_live, all_scale = client_lanes(
        count_ref, 0, count_ref.shape[0], span // image, (span // width) % slots, total
    )
    held = wide.shape[0]
    passes = [first for first in range(0, height, held)]

    def block_rows(h, lanes):
        return xall[h, :, :, lanes].reshape(LANES, -1)

    chosen = (
        lax.broadcasted_iota(jnp.int32, (mine // 9, channels), 1)
        == lax.broadcasted_iota(jnp.int32, (mine // 9, channels), 0) + own
    )
    chosen = jnp.where(chosen, 1.0, 0.0).astype(jnp.bfloat16)

    def own_rows(h):
        return lax.dot_general(
            chosen, block_rows(h, slice(None)), (((1,), (1,)), ((), ())), preferred_element_type=jnp.float32
        )

    for first in passes:
        spread(own_rows, all_live, mine // 9, wide, height, first, width)
        for chunk in range(held):
            mine_ref[:, (first + chunk) * LANES : (first + chunk + 1) * LANES] = (
                wide[chunk, :mine] * all_scale
            ).astype(jnp.bfloat16)

    tiles = gram_ref.shape[0]

    def fill(t, first, kept):
        lanes = pl.ds(pl.multiple_of(t * LANES, LANES), LANES)
        spread(lambda h: block_rows(h, lanes).astype(jnp.float32).T, all_live, LANES, wide, height, first, width)
        for chunk in range(held):
            kept[:, chunk * LANES : (chunk + 1) * LANES] = wide[chunk].astype(jnp.bfloat16)

    def product_of(t, first, kept):
        product = lax.dot_general(
            mine_ref[:, first * LANES : (first + held) * LANES], kept[...],
            (((1,), (1,)), ((), ())), preferred_element_type=jnp.float32,
        )
        if first != 0:
            product = product + gram_ref[t]
        if first == passes[-1]:
            where_diag = own * 9 - t * product.shape[1]
            on_diag = (
                lax.broadcasted_iota(jnp.int32, product.shape, 1)
                == lax.broadcasted_iota(jnp.int32, product.shape, 0) + where_diag
            )
            product = jnp.where(on_diag, product, keep_off * product)
        gram_ref[t] = product

    def happen(t, options):
        for when in options:
            if during[when]:
                pl.when(t == when)(functools.partial(run, during[when]))

    if len(passes) == 1 and tiles % 2 == 0:
        fill(0, 0, narrow)

        def pair(index, carry):
            t = index * 2
            happen(t, range(0, tiles, 2))
            product_of(t, 0, narrow)
            fill(t + 1, 0, narrow_next)
            happen(t + 1, range(1, tiles, 2))
            product_of(t + 1, 0, narrow_next)
            fill(jnp.minimum(t + 2, tiles - 1), 0, narrow)
            return carry

        lax.fori_loop(0, tiles // 2, pair, 0)
    else:

        def single(t, carry):
            happen(t, range(tiles))
            for first in passes:
                fill(t, first, narrow)
                product_of(t, first, narrow)
            return carry

        lax.fori_loop(0, tiles, single, 0)

    run(during[tiles])
    for q in range(pieces):
        settle(q)
    for entry in line:
        relay(*entry, wait_send, False)
    for entry in line:
        hand_over(*entry, wait_send, False)
    for d in range(1, blks):
        tile_copy(d).wait_send()
    for q in range(pieces):
        y_copy(q).wait_send()
        core_copy(q).wait_send()
        x_copy(q).wait_send()
        for d in range(1, depth):
            z_copy(q, d).wait_send()
            share(q, 0, d).wait_send()
        for d in range(depth):
            forward(q, d, y).wait_send()


def step_call(counts, x, weights, clients, blks, slots, width):
    stride, channels = x.shape
    groups, tall, columns = weights.shape
    mine = tall // clients
    tile = tall // 9
    height = blks
    pixels = height * stride
    everyone = clients * stride
    pieces = columns // PIECE if columns % PIECE == 0 else 1
    cols = columns // pieces
    depth = blks // 2
    held = min(KCHUNKS, height)
    sem = pltpu.SemaphoreType.DMA
    f32, bf16 = jnp.float32, jnp.bfloat16
    hop = pltpu.VMEM((pieces, depth, stride, cols), f32)
    return pl.pallas_call(
        functools.partial(step_kernel, groups, slots, width),
        in_specs=[
            pl.BlockSpec(memory_space=pltpu.SMEM),
            pl.BlockSpec(memory_space=pltpu.VMEM),
            pl.BlockSpec(memory_space=pltpu.HBM),
        ],
        out_specs=[pl.BlockSpec(memory_space=pltpu.VMEM)] * 2,
        out_shape=[
            pltpu.VMEM((channels // LANES, mine, LANES * 9), f32),
            pltpu.VMEM((mine, columns), f32),
        ],
        scratch_shapes=[
            pltpu.VMEM((blks, clients, stride, channels), bf16),
            pltpu.VMEM((blks, stride, tile), bf16),
            pltpu.VMEM((blks, stride, tile), bf16),
            pltpu.VMEM((tile, pixels), f32),
            pltpu.VMEM((pieces, groups, tall, cols), bf16),
            pltpu.VMEM((pixels // LANES, tall, LANES), f32),
            pltpu.VMEM((tall, pixels), bf16),
            pltpu.VMEM((tall, pixels), bf16),
            pltpu.VMEM((groups, pixels // groups, tall), bf16),
            pltpu.VMEM((groups, tall, LANES), f32),
            pltpu.VMEM((pieces, depth, 2, stride, cols), f32),
            hop,
            hop,
            hop,
            pltpu.VMEM((pieces, depth, 2, stride, cols), bf16),
            pltpu.VMEM((pieces, tall, cols), f32),
            pltpu.VMEM((pieces, 2, mine, cols), bf16),
            pltpu.VMEM((pieces, 2, mine, cols), bf16),
            pltpu.VMEM((pieces, mine, cols), bf16),
            pltpu.VMEM((pieces, mine, cols), bf16),
            pltpu.VMEM((held, LANES * 9, LANES), f32),
            pltpu.VMEM((LANES * 9, held * LANES), bf16),
            pltpu.VMEM((LANES * 9, held * LANES if height == held else LANES), bf16),
            pltpu.VMEM((mine, height * LANES), bf16),
            sem((blks,)),
            sem((blks,)),
            sem((5, clients * blks)),
            sem((clients * blks,)),
            sem((pieces,)),
            sem((pieces,)),
            sem((pieces,)),
        ]
        + [sem((pieces, depth))] * 6
        + [sem((pieces,))] * 4,
        compiler_params=pltpu.CompilerParams(
            collective_id=1, has_side_effects=True, vmem_limit_bytes=VMEM_MIB * 1024 * 1024
        ),
    )(counts, x, weights)


VMEM_MIB = 44


def store_kernel(gram_tiles, rhs_ref, gram_ref, out_ref, sems):
    tiles, rows, wide = gram_tiles.shape

    def tile_copy(t):
        return pltpu.make_async_copy(gram_tiles.at[t], gram_ref.at[:, pl.ds(t * wide, wide)], sems.at[t])

    rhs_copy = pltpu.make_async_copy(rhs_ref, out_ref, sems.at[tiles])
    for t in range(tiles):
        tile_copy(t).start()
    rhs_copy.start()
    for t in range(tiles):
        tile_copy(t).wait()
    rhs_copy.wait()


def store_call(gram_tiles, rhs):
    tiles, rows, wide = gram_tiles.shape
    return pl.pallas_call(
        store_kernel,
        in_specs=[pl.BlockSpec(memory_space=pltpu.VMEM)] * 2,
        out_specs=[pl.BlockSpec(memory_space=pl.ANY)] * 2,
        out_shape=[
            jax.ShapeDtypeStruct((rows, tiles * wide), jnp.float32),
            jax.ShapeDtypeStruct(rhs.shape, jnp.float32),
        ],
        scratch_shapes=[pltpu.SemaphoreType.DMA((tiles + 1,))],
        compiler_params=pltpu.CompilerParams(vmem_limit_bytes=24 * 1024 * 1024),
    )(gram_tiles, rhs)


def body(activations, sample_count, client_weights):
    blk_count = lax.axis_size("blk")
    group_size, slot_count, rows_here, width, channels = activations.shape
    client_groups = sample_count.shape[0] // group_size
    assert rows_here == 1 and client_groups * group_size * slot_count * width == LANES
    shard = activations.transpose(2, 0, 1, 3, 4).reshape(group_size * slot_count * width, channels)
    gram_tiles, rhs = step_call(
        sample_count, shard, client_weights, client_groups, blk_count, slot_count, width
    )
    return tuple(store_call(gram_tiles, rhs))


def solution(mesh):
    in_specs = (P("client", None, "blk", None, None), P(), P("client", "blk", None))
    out_specs = (P(("blk", "client"), None), P(("blk", "client"), None))
    return jax.shard_map(body, mesh=mesh, in_specs=in_specs, out_specs=out_specs, check_vma=False)
```

```python
import functools

import jax
import jax.numpy as jnp
from jax import lax
from jax.experimental import pallas as pl
from jax.experimental.pallas import tpu as pltpu
from jax.sharding import PartitionSpec as P

keep_off = 0.9
LANES = 128
KCHUNKS = 8


MESH = pl.DeviceIdType.MESH


def expand(base_of, live, channels, scratch, height, stride, width):
    pixels = live.shape[1]
    lane = lax.broadcasted_iota(jnp.int32, (1, pixels), 1)
    col = lane % width
    row = (lane // stride) % height

    def shifted(value, step, inside):
        return jnp.where(inside, pltpu.roll(value, (-step) % pixels, 1), 0.0)

    for first in range(0, channels, 16):
        size = min(16, channels - first)
        base = jnp.where(live > 0.0, base_of(first, size), 0.0)
        for b in range(3):
            if b == 1:
                across = base
            else:
                across = shifted(base, b - 1, (col + (b - 1) >= 0) & (col + (b - 1) < width))
            for a in range(3):
                if a == 1:
                    both = across
                else:
                    both = shifted(across, (a - 1) * stride, (row + (a - 1) >= 0) & (row + (a - 1) < height))
                for chunk in range(pixels // LANES):
                    scratch[chunk, pl.ds(first * 9 + 3 * a + b, size, stride=9), :] = both[
                        :, chunk * LANES : (chunk + 1) * LANES
                    ]


def spread(rows_of, live, channels, scratch, chunks, first_chunk, width):
    col = lax.broadcasted_iota(jnp.int32, (1, LANES), 1) % width
    held = scratch.shape[0]
    for h in range(max(first_chunk - 1, 0), min(first_chunk + held + 1, chunks)):
        value = rows_of(h)
        for first in range(0, channels, 8):
            size = min(8, channels - first)
            base = jnp.where(live > 0.0, value[first : first + size], 0.0)
            for b in range(3):
                if b == 1:
                    across = base
                else:
                    inside = (col + (b - 1) >= 0) & (col + (b - 1) < width)
                    across = jnp.where(inside, pltpu.roll(base, (1 - b) % LANES, 1), 0.0)
                for a in range(3):
                    to = h + 1 - a - first_chunk
                    if 0 <= to < held:
                        scratch[to, pl.ds(first * 9 + 3 * a + b, size, stride=9), :] = across
    for edge, a in ((0, 0), (chunks - 1, 2)):
        to = edge - first_chunk
        if 0 <= to < held:
            for first in range(0, channels, 8):
                size = min(8, channels - first)
                for b in range(3):
                    scratch[to, pl.ds(first * 9 + 3 * a + b, size, stride=9), :] = jnp.zeros(
                        (size, LANES), jnp.float32
                    )


START, GRAM, TILE, OVER = 12.5, 27.0, 1.9, 1.1
PIECE = 256


def plan(pieces, depth, part, tiles):
    listed = [(START + 0.46 * part * pieces, "damping")]
    for q in range(pieces):
        at = START + 0.45 * part * q
        listed.append((at, "multiply", q))
        listed.append((START + 0.47 * part * pieces + 0.5 * part * q, "damp", q))
        at = START + 1.5 + 2.8 * part * (q + 1)
        listed.append((at, "add_y", q))
        for name, wait in (
            ("add_z", 2.8 * part + 2.5), ("pass_on", 1.4 * part + 2.5),
            ("cross", 1.4 * part + 1.5), ("finish", 0.8 * part + 1.7),
        ):
            at += wait
            listed.append((at, name, q))
    for index in range(4 * depth - 2):
        distance = (index + 2) // 4
        at = START - 1.0 + 2.2 * (distance - 1) + 1.5 * (index % 4 in (0, 1) if distance else index)
        if index > 3:
            listed.append((at, "relay", index))
        if index:
            listed.append((max(at + 3.0, START - 0.5 + OVER * index), "over", index))
    listed.sort(key=lambda entry: entry[0])
    before = [entry[1:] for entry in listed if entry[0] < GRAM or entry[1] in ("relay", "over")]
    during = [[] for _ in range(tiles + 1)]
    for at, *entry in listed:
        if tuple(entry) not in before:
            during[min(int((at - GRAM) / TILE), tiles)].append(tuple(entry))
    return before, during


def client_lanes(count_ref, first, clients, client, slot, total):
    count = jnp.zeros(client.shape, jnp.int32)
    for index in range(clients):
        count = jnp.where(client == index, count_ref[first + index], count)
    live = jnp.where(slot < count, 1.0, 0.0)
    return live, 1.0 / (total * count.astype(jnp.float32))


def step_kernel(
    groups, slots, width, count_ref, x_ref, w_ref, gram_ref, rhs_ref,
    xall, tsend, trecv, flat, wbuf, tall_wide, patch, scaled, across, square,
    part_ref, ybuf, sums, zbuf, obuf, rbuf, abuf, cbuf, vbuf, ubuf, wide, narrow, narrow_next, mine_ref,
    tss, tsr, hs, hr, ws, ys, yr, zs, zr, gs, gr, fs, fr, cs, cr, vs, vr,
):
    blks, clients, stride, channels = xall.shape
    height = blks
    pieces, depth = part_ref.shape[:2]
    cols = part_ref.shape[4]
    tile = trecv.shape[2]
    tall = tall_wide.shape[1]
    pixels = height * stride
    image = slots * width
    mine = rhs_ref.shape[0]
    total = count_ref.shape[0] * height * width
    client, blk = lax.axis_index("client"), lax.axis_index("blk")
    z, y = blk // 2, blk % 2
    core, side = client % 2, client // 2
    other = 1 - y
    core_mate = client + 1 - 2 * core
    x_mate = (client + 2) % clients
    core_dev, x_dev, y_dev = (core_mate, blk), (x_mate, blk), (client, blk + 1 - 2 * y)
    up_dev, down_dev = (client, blk + 2), (client, blk - 2)

    def level(d):
        return (z + d) % depth

    def z_dev(d):
        return (client, level(d) * 2 + y)

    def near(d):
        return (blk + d) % blks

    def w_copy(q):
        return pltpu.make_async_copy(w_ref.at[:, :, pl.ds(q * cols, cols)], wbuf.at[q], ws.at[q])

    for q in range(pieces):
        w_copy(q).start()

    barrier = pltpu.get_barrier_semaphore()
    for device in [core_dev, x_dev] + [(client, near(d)) for d in range(1, blks)]:
        pl.semaphore_signal(barrier, inc=1, device_id=device, device_id_type=MESH)
    for b in range(blks):
        tsend[b] = x_ref[:, b * tile : (b + 1) * tile]
    xall[blk, client] = x_ref[...]
    pl.semaphore_wait(barrier, blks + 1)

    def send(src, dst, send_sem, recv_sem, device):
        return pltpu.make_async_remote_copy(
            src_ref=src, dst_ref=dst, send_sem=send_sem, recv_sem=recv_sem, device_id=device, device_id_type=MESH
        )

    def tile_copy(d):
        return send(tsend.at[near(d)], trecv.at[blk], tss.at[d], tsr.at[blk], (client, near(d)))

    def tile_arrival(d):
        here = trecv.at[near(d)]
        return send(here, here, tss.at[d], tsr.at[near(d)], (client, near(d)))

    def hop(lane, c, b, device, own=False):
        dst = xall.at[b, c]
        src = x_ref if own else dst
        return send(src, dst, hs.at[lane, c * blks + b], hr.at[c * blks + b], device)

    def relay(d, mate, act, arrive=True):
        own = d == 0 and not mate

        def forward_block():
            b = (z + d) * 2 + (other if mate else y)
            if arrive and not own:
                hop(0, client, b, core_dev).wait_recv()
            if d != 0 or not mate:
                act(hop(2, client, b, x_dev, own))
            if own:
                act(hop(3, client, b, y_dev, own))
            if d <= 0:
                pl.when(z + 1 < depth)(lambda: act(hop(0, client, b, up_dev, own)))
            if d >= 0:
                pl.when(z > 0)(lambda: act(hop(1, client, b, down_dev, own)))
            act(hop(4, client, b, core_dev, own))

        if d == 0:
            forward_block()
        else:
            pl.when((z + d >= 0) & (z + d < depth))(forward_block)

    def hand_over(d, mate, act, arrive=True):
        def pass_block():
            b = (z + d) * 2 + (other if mate else y)
            if arrive:
                hop(2, x_mate, b, core_dev).wait_recv()
            if d == 0 and not mate:
                act(hop(3, x_mate, b, y_dev))
            act(hop(4, x_mate, b, core_dev))

        if d == 0:
            pass_block()
        else:
            pl.when((z + d >= 0) & (z + d < depth))(pass_block)

    def start(copy):
        copy.start()

    def wait_send(copy):
        copy.wait_send()

    line = [(0, False), (0, True)]
    for distance in range(1, depth):
        line += [(-distance, False), (distance, False), (-distance, True), (distance, True)]

    for d in range(1, blks):
        tile_copy(d).start()
    relay(0, False, start)

    def y_copy(q):
        return send(part_ref.at[q, :, other], ybuf.at[q], ys.at[q], yr.at[q], y_dev)

    def z_copy(q, d):
        return send(sums.at[q, level(d)], zbuf.at[q, d], zs.at[q, d], zr.at[q, d], z_dev(d))

    def share(q, d, to):
        here = obuf.at[q, level(d), y]
        return send(here, here, gs.at[q, to], gr.at[q, to], z_dev(to))

    def forward(q, d, column):
        here = obuf.at[q, level(d), column]
        return send(here, here, fs.at[q, d], fr.at[q, level(d)], y_dev)

    def core_copy(q):
        return send(abuf.at[q], cbuf.at[q], cs.at[q], cr.at[q], core_dev)

    def x_copy(q):
        return send(vbuf.at[q], ubuf.at[q], vs.at[q], vr.at[q], x_dev)

    lane = lax.broadcasted_iota(jnp.int32, (1, pixels), 1)
    who = (lane // image) % groups
    live, scale = client_lanes(count_ref, client * groups, groups, who, (lane // width) % slots, total)

    def patches():
        trecv[blk] = tsend[blk]
        for d in range(1, blks):
            tile_arrival(d).wait_recv()
        for index in range(1, 4):
            relay(*line[index], start)
        hand_over(*line[0], start)
        flat[...] = trecv[...].reshape(pixels, tile).astype(jnp.float32).T
        expand(lambda first, size: flat[first : first + size, :], live, tile, tall_wide, height, stride, width)
        for chunk in range(tall_wide.shape[0]):
            span = slice(chunk * LANES, (chunk + 1) * LANES)
            value = tall_wide[chunk]
            patch[:, span] = value.astype(jnp.bfloat16)
            scaled[:, span] = (value * scale[:, span]).astype(jnp.bfloat16)
        flipped = patch[...].T
        for h in range(height):
            for group in range(groups):
                across[group, h * image : (h + 1) * image] = flipped[
                    (h * groups + group) * image : (h * groups + group + 1) * image
                ]

    def multiply(q):
        w_copy(q).wait()
        for group in range(groups):
            term = jnp.dot(across[group], wbuf[q, group], preferred_element_type=jnp.float32)
            for h in range(height):
                part_ref[q, h // 2, h % 2, group * image : (group + 1) * image] = term[h * image : (h + 1) * image]
        y_copy(q).start()

    def damping():
        for group in range(groups):
            term = jnp.zeros((tall, 1), jnp.float32)
            for chunk in range(tall_wide.shape[0]):
                span = slice(chunk * LANES, (chunk + 1) * LANES)
                value = tall_wide[chunk]
                value = jnp.where(who[:, span] == group, value * value * scale[:, span], 0.0)
                term += jnp.sum(value, axis=1, keepdims=True)
            square[group] = jnp.broadcast_to(term * (1.0 - keep_off), (tall, LANES))

    def damp(q):
        rows = 80 if tall % 80 == 0 else tall

        def block(index, carry):
            span = pl.ds(pl.multiple_of(index * rows, 8), rows)
            for first in range(0, cols, LANES):
                total = None
                for group in range(groups):
                    term = square[group, span, :] * wbuf[q, group, span, first : first + LANES].astype(jnp.float32)
                    total = term if total is None else total + term
                rbuf[q, span, first : first + LANES] = total
            return carry

        lax.fori_loop(0, tall // rows, block, 0)

    def add_y(q):
        y_copy(q).wait_recv()
        for d in range(depth):
            sums[q, level(d)] = part_ref[q, level(d), y] + ybuf[q, level(d)]
        for d in range(1, depth):
            z_copy(q, d).start()

    def add_z(q):
        total = sums[q, z]
        for d in range(1, depth):
            z_copy(q, d).wait_recv()
            total = total + zbuf[q, d]
        obuf[q, z, y] = total.astype(jnp.bfloat16)
        for d in range(1, depth):
            share(q, 0, d).start()
        forward(q, 0, y).start()

    def pass_on(q):
        for d in range(1, depth):
            share(q, depth - d, d).wait_recv()
            forward(q, depth - d, y).start()

    def rows_of(q, holder):
        if mine % 8 == 0:
            return rbuf[q, pl.ds(pl.multiple_of(holder * mine, 8), mine), :]
        value = rbuf[q, :mine, :]
        for index in range(1, tall // mine):
            value = jnp.where(holder == index, rbuf[q, index * mine : (index + 1) * mine, :], value)
        return value

    def cross(q):
        for d in range(depth):
            forward(q, d, other).wait_recv()
        product = jnp.dot(scaled[...], obuf[q].reshape(pixels, cols), preferred_element_type=jnp.float32)
        rbuf[q] = rbuf[q] + keep_off * product
        for far in range(2):
            abuf[q, far] = rows_of(q, far * 2 + 1 - core).astype(jnp.bfloat16)
        core_copy(q).start()

    def finish(q):
        core_copy(q).wait_recv()
        far = 1 - side
        away = rows_of(q, far * 2 + core) + cbuf[q, far].astype(jnp.float32)
        vbuf[q] = away.astype(jnp.bfloat16)
        x_copy(q).start()
        span = slice(q * cols, (q + 1) * cols)
        rhs_ref[:, span] = rows_of(q, client) + cbuf[q, side].astype(jnp.float32)

    def settle(q):
        x_copy(q).wait_recv()
        span = slice(q * cols, (q + 1) * cols)
        rhs_ref[:, span] = rhs_ref[:, span] + ubuf[q].astype(jnp.float32)

    actions = {
        "multiply": multiply,
        "damping": damping,
        "damp": damp,
        "add_y": add_y,
        "add_z": add_z,
        "pass_on": pass_on,
        "cross": cross,
        "finish": finish,
        "relay": lambda index: relay(*line[index], start),
        "over": lambda index: hand_over(*line[index], start),
    }

    def run(listed):
        for name, *values in listed:
            actions[name](*values)

    before, during = plan(pieces, depth, cols / 256, gram_ref.shape[0])
    patches()
    run(before)
    far_mate = (core_mate + 2) % clients
    for b in range(blks):
        for c in (core_mate, far_mate):
            hop(4, c, b, core_dev).wait_recv()

    own = blk * tile + client * (mine // 9)
    span = lax.broadcasted_iota(jnp.int32, (1, LANES), 1)
    all_live, all_scale = client_lanes(
        count_ref, 0, count_ref.shape[0], span // image, (span // width) % slots, total
    )
    held = wide.shape[0]
    passes = [first for first in range(0, height, held)]

    def block_rows(h, lanes):
        return xall[h, :, :, lanes].reshape(LANES, -1)

    chosen = (
        lax.broadcasted_iota(jnp.int32, (mine // 9, channels), 1)
        == lax.broadcasted_iota(jnp.int32, (mine // 9, channels), 0) + own
    )
    chosen = jnp.where(chosen, 1.0, 0.0).astype(jnp.bfloat16)

    def own_rows(h):
        return lax.dot_general(
            chosen, block_rows(h, slice(None)), (((1,), (1,)), ((), ())), preferred_element_type=jnp.float32
        )

    for first in passes:
        spread(own_rows, all_live, mine // 9, wide, height, first, width)
        for chunk in range(held):
            mine_ref[:, (first + chunk) * LANES : (first + chunk + 1) * LANES] = (
                wide[chunk, :mine] * all_scale
            ).astype(jnp.bfloat16)

    tiles = gram_ref.shape[0]

    def fill(t, first, kept):
        lanes = pl.ds(pl.multiple_of(t * LANES, LANES), LANES)
        spread(lambda h: block_rows(h, lanes).astype(jnp.float32).T, all_live, LANES, wide, height, first, width)
        for chunk in range(held):
            kept[:, chunk * LANES : (chunk + 1) * LANES] = wide[chunk].astype(jnp.bfloat16)

    def product_of(t, first, kept):
        product = lax.dot_general(
            mine_ref[:, first * LANES : (first + held) * LANES], kept[...],
            (((1,), (1,)), ((), ())), preferred_element_type=jnp.float32,
        )
        if first != 0:
            product = product + gram_ref[t]
        if first == passes[-1]:
            where_diag = own * 9 - t * product.shape[1]
            on_diag = (
                lax.broadcasted_iota(jnp.int32, product.shape, 1)
                == lax.broadcasted_iota(jnp.int32, product.shape, 0) + where_diag
            )
            product = jnp.where(on_diag, product, keep_off * product)
        gram_ref[t] = product

    def happen(t, options):
        for when in options:
            if during[when]:
                pl.when(t == when)(functools.partial(run, during[when]))

    if len(passes) == 1 and tiles % 2 == 0:
        fill(0, 0, narrow)

        def pair(index, carry):
            t = index * 2
            happen(t, range(0, tiles, 2))
            product_of(t, 0, narrow)
            fill(t + 1, 0, narrow_next)
            happen(t + 1, range(1, tiles, 2))
            product_of(t + 1, 0, narrow_next)
            fill(jnp.minimum(t + 2, tiles - 1), 0, narrow)
            return carry

        lax.fori_loop(0, tiles // 2, pair, 0)
    else:

        def single(t, carry):
            happen(t, range(tiles))
            for first in passes:
                fill(t, first, narrow)
                product_of(t, first, narrow)
            return carry

        lax.fori_loop(0, tiles, single, 0)

    run(during[tiles])
    for q in range(pieces):
        settle(q)
    for entry in line:
        relay(*entry, wait_send, False)
    for entry in line:
        hand_over(*entry, wait_send, False)
    for d in range(1, blks):
        tile_copy(d).wait_send()
    for q in range(pieces):
        y_copy(q).wait_send()
        core_copy(q).wait_send()
        x_copy(q).wait_send()
        for d in range(1, depth):
            z_copy(q, d).wait_send()
            share(q, 0, d).wait_send()
        for d in range(depth):
            forward(q, d, y).wait_send()


def step_call(counts, x, weights, clients, blks, slots, width):
    stride, channels = x.shape
    groups, tall, columns = weights.shape
    mine = tall // clients
    tile = tall // 9
    height = blks
    pixels = height * stride
    everyone = clients * stride
    pieces = columns // PIECE if columns % PIECE == 0 else 1
    cols = columns // pieces
    depth = blks // 2
    held = min(KCHUNKS, height)
    sem = pltpu.SemaphoreType.DMA
    f32, bf16 = jnp.float32, jnp.bfloat16
    hop = pltpu.VMEM((pieces, depth, stride, cols), f32)
    return pl.pallas_call(
        functools.partial(step_kernel, groups, slots, width),
        in_specs=[
            pl.BlockSpec(memory_space=pltpu.SMEM),
            pl.BlockSpec(memory_space=pltpu.VMEM),
            pl.BlockSpec(memory_space=pltpu.HBM),
        ],
        out_specs=[pl.BlockSpec(memory_space=pltpu.VMEM)] * 2,
        out_shape=[
            pltpu.VMEM((channels // LANES, mine, LANES * 9), f32),
            pltpu.VMEM((mine, columns), f32),
        ],
        scratch_shapes=[
            pltpu.VMEM((blks, clients, stride, channels), bf16),
            pltpu.VMEM((blks, stride, tile), bf16),
            pltpu.VMEM((blks, stride, tile), bf16),
            pltpu.VMEM((tile, pixels), f32),
            pltpu.VMEM((pieces, groups, tall, cols), bf16),
            pltpu.VMEM((pixels // LANES, tall, LANES), f32),
            pltpu.VMEM((tall, pixels), bf16),
            pltpu.VMEM((tall, pixels), bf16),
            pltpu.VMEM((groups, pixels // groups, tall), bf16),
            pltpu.VMEM((groups, tall, LANES), f32),
            pltpu.VMEM((pieces, depth, 2, stride, cols), f32),
            hop,
            hop,
            hop,
            pltpu.VMEM((pieces, depth, 2, stride, cols), bf16),
            pltpu.VMEM((pieces, tall, cols), f32),
            pltpu.VMEM((pieces, 2, mine, cols), bf16),
            pltpu.VMEM((pieces, 2, mine, cols), bf16),
            pltpu.VMEM((pieces, mine, cols), bf16),
            pltpu.VMEM((pieces, mine, cols), bf16),
            pltpu.VMEM((held, LANES * 9, LANES), f32),
            pltpu.VMEM((LANES * 9, held * LANES), bf16),
            pltpu.VMEM((LANES * 9, held * LANES if height == held else LANES), bf16),
            pltpu.VMEM((mine, height * LANES), bf16),
            sem((blks,)),
            sem((blks,)),
            sem((5, clients * blks)),
            sem((clients * blks,)),
            sem((pieces,)),
            sem((pieces,)),
            sem((pieces,)),
        ]
        + [sem((pieces, depth))] * 6
        + [sem((pieces,))] * 4,
        compiler_params=pltpu.CompilerParams(
            collective_id=1, has_side_effects=True, vmem_limit_bytes=VMEM_MIB * 1024 * 1024
        ),
    )(counts, x, weights)


VMEM_MIB = 44


def store_kernel(gram_tiles, rhs_ref, gram_ref, out_ref, sems):
    tiles, rows, wide = gram_tiles.shape

    def tile_copy(t):
        return pltpu.make_async_copy(gram_tiles.at[t], gram_ref.at[:, pl.ds(t * wide, wide)], sems.at[t])

    rhs_copy = pltpu.make_async_copy(rhs_ref, out_ref, sems.at[tiles])
    for t in range(tiles):
        tile_copy(t).start()
    rhs_copy.start()
    for t in range(tiles):
        tile_copy(t).wait()
    rhs_copy.wait()


def store_call(gram_tiles, rhs):
    tiles, rows, wide = gram_tiles.shape
    return pl.pallas_call(
        store_kernel,
        in_specs=[pl.BlockSpec(memory_space=pltpu.VMEM)] * 2,
        out_specs=[pl.BlockSpec(memory_space=pl.ANY)] * 2,
        out_shape=[
            jax.ShapeDtypeStruct((rows, tiles * wide), jnp.float32),
            jax.ShapeDtypeStruct(rhs.shape, jnp.float32),
        ],
        scratch_shapes=[pltpu.SemaphoreType.DMA((tiles + 1,))],
        compiler_params=pltpu.CompilerParams(vmem_limit_bytes=24 * 1024 * 1024),
    )(gram_tiles, rhs)


def body(activations, sample_count, client_weights):
    blk_count = lax.axis_size("blk")
    group_size, slot_count, rows_here, width, channels = activations.shape
    client_groups = sample_count.shape[0] // group_size
    assert rows_here == 1 and client_groups * group_size * slot_count * width == LANES
    shard = activations.transpose(2, 0, 1, 3, 4).reshape(group_size * slot_count * width, channels)
    gram_tiles, rhs = step_call(
        sample_count, shard, client_weights, client_groups, blk_count, slot_count, width
    )
    return tuple(store_call(gram_tiles, rhs))


def solution(mesh):
    in_specs = (P("client", None, "blk", None, None), P(), P("client", "blk", None))
    out_specs = (P(("blk", "client"), None), P(("blk", "client"), None))
    return jax.shard_map(body, mesh=mesh, in_specs=in_specs, out_specs=out_specs, check_vma=False)
```
